32 devices in a mesh: pair: 4 (over y, x), vtile: 8 (over z, core).
Axes of the slice: x: 2, y: 2, z: 4, core: 2. Of those that a mesh axis runs over, the one named last changes fastest.
Arguments:
- amplitudes: bfloat16 [32, 512, 512], P(('pair', 'vtile')), may hold values from -1.1953125 to 1.1953125
- factors: bfloat16 [512, 512, 2048], P('vtile', 'pair'), may hold values from -0.125 to 0.125
- pair_list: int32 [32, 2], P(('pair', 'vtile')), may hold values from 0 to 127
- window_offsets: int32 [2], replicated, may hold values from 0 to 511
- occupied_energy: float32 [128], replicated, may hold values from -3 to -0.5
- virtual_energy: float32 [512], replicated, may hold values from 0.5 to 4
Outputs:
- residual: float32 [32, 2, 512], P(('pair', 'vtile'))
- update: float32 [32, 2, 512], P(('pair', 'vtile'))
The draws below stay inside these ranges and needn't reach their ends.
All inputs are finite; a program needn't handle non-finite values.
Results may differ from the reference program's by a relative error of at most 0.0029.
Values may be sent and summed in bfloat16 or wider, within the bound.
A program may use at most 128 MiB of HBM per device.

```python
import math
import jax
import jax.numpy as jnp
from jax import lax

OCC = 128
VIRT = 512
AUX = 2048
AWIN = 2
PAIRS = 32


def with_ends(entries, stream_key, low, largest):
    spot = [jax.random.randint(jax.random.fold_in(stream_key, axis), (), 0, length) for axis, length in enumerate(entries.shape)]
    widest = entries.shape.index(max(entries.shape))
    next_to = spot[:widest] + [(spot[widest] + 1) % entries.shape[widest]] + spot[widest + 1:]
    return entries.at[tuple(spot)].set(low).at[tuple(next_to)].set(largest)


def shard_levels(own_key, dims, cuts, least, top_value):
    factor_of = 1.0
    for position, parts in cuts:
        heights = jax.random.uniform(jax.random.fold_in(jax.random.fold_in(own_key, 6), position), (parts,), jnp.float32, least / len(cuts), top_value / len(cuts))
        factor_of = factor_of * jnp.repeat(jnp.exp(heights), dims[position] // parts).reshape((-1,) + (1,) * (len(dims) - 1 - position))
    return factor_of


def gaussian(own_key, dims, spread, reach, cuts=(), kind=jnp.bfloat16):
    factor_of = shard_levels(own_key, dims, cuts, -0.22, 0.18) if cuts else 1.0
    drawn = jax.random.normal(own_key, dims, jnp.float32) * spread * factor_of
    return jnp.minimum(jnp.maximum(drawn, -reach), reach).astype(kind)


def setup_inputs(seed: int = 0) -> dict:
    arg_keys = jax.random.split(jax.random.key(seed), 7)
    return {
        "amplitudes": gaussian(arg_keys[0], (PAIRS, VIRT, VIRT), 0.2, 1.1953125, ((0, 32),)),
        "factors": gaussian(arg_keys[1], (VIRT, VIRT, AUX), AUX ** -0.5, 0.125, ((0, 8), (1, 4))),
        "pair_list": with_ends(jax.random.randint(arg_keys[2], (PAIRS, 2), 0, OCC), jax.random.fold_in(arg_keys[2], 1), 0, OCC - 1).astype(jnp.int32),
        "window_offsets": jax.random.randint(arg_keys[3], (AWIN,), 0, VIRT).astype(jnp.int32),
        "occupied_energy": jnp.clip(jax.random.uniform(arg_keys[4], (OCC,), jnp.float32, -3.0, -0.5), -3.0, -0.5),
        "virtual_energy": jnp.clip(jnp.exp(jax.random.uniform(arg_keys[5], (VIRT,), jnp.float32, math.log(0.5), math.log(4.0))), 0.5, 4.0),
    }


def reference(amplitudes, factors, pair_list, window_offsets, occupied_energy, virtual_energy):
    width = min(64, VIRT)
    arows = factors[window_offsets]
    left_side = arows.reshape(AWIN * VIRT, AUX)

    def one_range(range_index):
        offset = (range_index * width).astype(jnp.int32)
        slab = lax.dynamic_slice_in_dim(factors, offset, width, 1)
        integrals = jnp.dot(left_side, slab.reshape(VIRT * width, AUX).T, preferred_element_type=jnp.float32).astype(jnp.bfloat16)
        integrals = integrals.reshape(AWIN, VIRT, VIRT, width).transpose(0, 2, 1, 3).reshape(AWIN * VIRT, VIRT * width)
        tau_slab = lax.dynamic_slice_in_dim(amplitudes, offset, width, 2).reshape(PAIRS, VIRT * width)
        return jnp.dot(tau_slab, integrals.T, preferred_element_type=jnp.float32)

    pieces = lax.map(one_range, jnp.arange(VIRT // width, dtype=jnp.int32))
    residual = jnp.sum(pieces, axis=0).reshape(PAIRS, AWIN, VIRT)
    occupied_sum = occupied_energy[pair_list[:, 0]] + occupied_energy[pair_list[:, 1]]
    window_energy = virtual_energy[window_offsets]
    denominator = window_energy[None, :, None] + virtual_energy[None, None, :] - occupied_sum[:, None, None]
    update = residual / denominator
    return residual, update
```

```python
import functools

import jax
import jax.numpy as jnp
from jax import lax
from jax.experimental import pallas as pl
from jax.experimental.pallas import tpu as pltpu
from jax.sharding import PartitionSpec as P

MESH = pl.DeviceIdType.MESH


def lookup(table, indices):
    positions = jnp.arange(table.shape[0], dtype=jnp.int32)
    return jnp.sum(jnp.where(positions[None, :] == indices[:, None], table[None, :], 0.0), axis=1)


def spread_kernel(
    pair_count, tile_count, sub,
    rows_ref, amp_ref, full_ref, mine_ref,
    core_buf, own_buf, up_buf, down_buf, up_out, down_out,
    core_sems, up_sems, down_sems, peer_sems, fwd_sems, amp_sems, local_sem,
):
    p = lax.axis_index("pair")
    t = lax.axis_index("vtile")
    core = lax.rem(t, 2)
    stage = t // 2
    stages = tile_count // 2
    window, cols, aux = rows_ref.shape
    half = aux // 2
    mate = (p, stage * 2 + (1 - core))
    above = (p, t + 2)
    below = (p, t - 2)
    peers = [(lax.rem(p + j, pair_count), t) for j in range(1, pair_count)]
    sources = [lax.rem(p + pair_count - j, pair_count) for j in range(1, pair_count)]

    barrier = pltpu.get_barrier_semaphore()
    around = [(p, lax.rem(t + 2, tile_count)), (p, lax.rem(t + tile_count - 2, tile_count))]
    for device in [mate] + peers + around:
        pl.semaphore_signal(barrier, inc=1, device_id=device, device_id_type=MESH)
    pl.semaphore_wait(barrier, pair_count + 2)

    mine_lanes = pl.ds(pl.multiple_of(core * half, half), half)
    mate_lanes = pl.ds(pl.multiple_of((1 - core) * half, half), half)
    chunks = [(k, pl.ds(s * sub, sub)) for k in range(window) for s in range(cols // sub)]
    count = len(chunks)

    def remote(src, dst, sems, index, device):
        return pltpu.make_async_remote_copy(
            src_ref=src, dst_ref=dst, send_sem=sems.at[(0,) + index], recv_sem=sems.at[(1,) + index],
            device_id=device, device_id_type=MESH,
        )

    def core_copy(h):
        k, rows = chunks[h]
        return remote(rows_ref.at[k, rows, mate_lanes], core_buf.at[k, rows], core_sems, (h,), mate)

    def up_copy(h):
        k, rows = chunks[h]
        return remote(up_out.at[k, rows], up_buf.at[k, rows], up_sems, (h,), above)

    def down_copy(h):
        k, rows = chunks[h]
        return remote(down_out.at[k, rows], down_buf.at[k, rows], down_sems, (h,), below)

    def peer_copy(h, j):
        k, rows = chunks[h]
        place = full_ref.at[k, p, rows, mine_lanes]
        return remote(place, place, peer_sems, (j, h), peers[j])

    def fwd_copy(h, j):
        k, rows = chunks[h]
        source = p if j == pair_count - 1 else sources[j]
        place = full_ref.at[k, source, rows, mine_lanes]
        return remote(place, place, fwd_sems, (j, h), mate)

    def amp_copy(j):
        return remote(amp_ref.at[peers[j][0]], mine_ref.at[p], amp_sems, (j,), peers[j])

    for h in range(count):
        core_copy(h).start()
    for j in range(pair_count - 1):
        amp_copy(j).start()
    keep = pltpu.make_async_copy(amp_ref.at[p], mine_ref.at[p], local_sem)
    keep.start()

    def combine(h):
        k, rows = chunks[h]
        core_copy(h).wait_recv()
        own_buf[k, rows, :] = rows_ref[k, rows, mine_lanes] + core_buf[k, rows, :]

        @pl.when(stage == 0)
        def _():
            up_out[k, rows, :] = own_buf[k, rows, :]
            up_copy(h).start()

        @pl.when(stage == stages - 1)
        def _():
            down_out[k, rows, :] = own_buf[k, rows, :]
            down_copy(h).start()

    def go_up(h):
        k, rows = chunks[h]

        @pl.when(stage > 0)
        def _():
            up_copy(h).wait_recv()

            @pl.when(stage < stages - 1)
            def _():
                up_out[k, rows, :] = own_buf[k, rows, :] + up_buf[k, rows, :]
                up_copy(h).start()

    def go_down(h):
        k, rows = chunks[h]

        @pl.when(stage < stages - 1)
        def _():
            down_copy(h).wait_recv()

            @pl.when(stage > 0)
            def _():
                down_out[k, rows, :] = own_buf[k, rows, :] + down_buf[k, rows, :]
                down_copy(h).start()

    def finish(h):
        k, rows = chunks[h]

        @pl.when(stage == 0)
        def _():
            full_ref[k, p, rows, mine_lanes] = own_buf[k, rows, :] + down_buf[k, rows, :]

        @pl.when(stage == stages - 1)
        def _():
            full_ref[k, p, rows, mine_lanes] = own_buf[k, rows, :] + up_buf[k, rows, :]

        @pl.when(jnp.logical_and(stage > 0, stage < stages - 1))
        def _():
            full_ref[k, p, rows, mine_lanes] = (
                own_buf[k, rows, :] + up_buf[k, rows, :] + down_buf[k, rows, :]
            )

        for j in range(pair_count - 1):
            peer_copy(h, j).start()
        fwd_copy(h, pair_count - 1).start()

    def forward(h):
        for j in range(pair_count - 1):
            peer_copy(h, j).wait_recv()
            fwd_copy(h, j).start()

    for h in range(count):
        combine(h)
    lag = 3
    for step in range(count + lag):
        if step < count:
            go_up(step)
            go_down(step)
            finish(step)
        if step >= lag:
            forward(step - lag)
    for h in range(count):
        core_copy(h).wait_send()

        @pl.when(stage < stages - 1)
        def _():
            up_copy(h).wait_send()

        @pl.when(stage > 0)
        def _():
            down_copy(h).wait_send()

        for j in range(pair_count - 1):
            peer_copy(h, j).wait_send()
        for j in range(pair_count):
            fwd_copy(h, j).wait()
    for j in range(pair_count - 1):
        amp_copy(j).wait()
    keep.wait()


def spread(picked, amp, pair_count, tile_count):
    window, cols, aux = picked.shape
    half = aux // 2
    sub = max(16, cols // 4)
    count = window * cols // sub
    block = pltpu.VMEM((window, cols, half), picked.dtype)
    dma = pltpu.SemaphoreType.DMA
    vmem = pl.BlockSpec(memory_space=pltpu.VMEM)
    return pl.pallas_call(
        functools.partial(spread_kernel, pair_count, tile_count, sub),
        out_shape=(
            jax.ShapeDtypeStruct((window, pair_count, cols, aux), picked.dtype),
            jax.ShapeDtypeStruct(amp.shape, amp.dtype),
        ),
        in_specs=[vmem, vmem],
        out_specs=(vmem, vmem),
        scratch_shapes=[block] * 6
        + [
            dma((2, count)), dma((2, count)), dma((2, count)),
            dma((2, pair_count - 1, count)), dma((2, pair_count, count)),
            dma((2, pair_count - 1)), dma,
        ],
        compiler_params=pltpu.CompilerParams(
            collective_id=0, has_side_effects=True, vmem_limit_bytes=32 * 1024 * 1024
        ),
    )(picked, amp)


def settle_kernel(pair_count, tile_count, part_ref, sum_ref, inbox, sems, local_sem):
    p = lax.axis_index("pair")
    t = lax.axis_index("vtile")
    total = pair_count * tile_count
    me = p * tile_count + t
    barrier = pltpu.get_barrier_semaphore()

    def place(offset):
        other = lax.rem(me + offset, total)
        return other // tile_count, lax.rem(other, tile_count)

    for offset in range(1, total):
        pl.semaphore_signal(barrier, inc=1, device_id=place(offset), device_id_type=MESH)
    pl.semaphore_wait(barrier, total - 1)

    def copy(offset):
        there = place(offset)
        return pltpu.make_async_remote_copy(
            src_ref=part_ref.at[there[1], there[0]], dst_ref=inbox.at[p, t],
            send_sem=sems.at[0, offset], recv_sem=sems.at[1, offset],
            device_id=there, device_id_type=MESH,
        )

    for offset in range(1, total):
        copy(offset).start()
    keep = pltpu.make_async_copy(part_ref.at[t, p], inbox.at[p, t], local_sem)
    keep.start()
    keep.wait()
    for offset in range(1, total):
        copy(offset).wait()
    added = inbox[0]
    for source in range(1, pair_count):
        added = added + inbox[source]
    sum_ref[...] = added


def settle(part):
    tile_count, pair_count, local_pairs, width = part.shape
    total = tile_count * pair_count
    vmem = pl.BlockSpec(memory_space=pltpu.VMEM)
    return pl.pallas_call(
        functools.partial(settle_kernel, pair_count, tile_count),
        out_shape=jax.ShapeDtypeStruct((tile_count, local_pairs, width), part.dtype),
        in_specs=[vmem],
        out_specs=vmem,
        scratch_shapes=[
            pltpu.VMEM((pair_count, tile_count, local_pairs, width), part.dtype),
            pltpu.SemaphoreType.DMA((2, total)),
            pltpu.SemaphoreType.DMA,
        ],
        compiler_params=pltpu.CompilerParams(collective_id=1, has_side_effects=True),
    )(part)


def local(amplitudes, factors, pair_list, window_offsets, occupied_energy, virtual_energy):
    pair_count = lax.axis_size("pair")
    tile_count = lax.axis_size("vtile")
    row_count, col_count, aux_count = factors.shape
    window_count = window_offsets.shape[0]
    local_pairs, virt_count = (amplitudes.shape[0], amplitudes.shape[1])
    local_rows = window_offsets % row_count
    owned = (window_offsets // row_count) == lax.axis_index("vtile")
    picked = jnp.stack(
        [
            lax.dynamic_index_in_dim(factors, local_rows[slot_index], 0, keepdims=False)
            for slot_index in range(window_count)
        ]
    )
    picked = jnp.where(owned[:, None, None], picked, jnp.zeros_like(picked))
    amp = amplitudes.reshape(local_pairs, virt_count, pair_count, col_count).transpose(2, 0, 1, 3)
    arows, mine = spread(picked, amp, pair_count, tile_count)
    arows = arows.reshape(window_count, virt_count, aux_count)
    mine = mine.reshape(pair_count * local_pairs, virt_count, col_count)
    section = lax.all_gather(mine, "vtile", axis=0, tiled=True)
    integrals = jnp.einsum(
        "acq,bdq->abcd", arows, factors, preferred_element_type=jnp.float32
    ).astype(jnp.bfloat16)
    kernel = integrals.reshape(window_count * row_count, virt_count * col_count)
    flat = section.reshape(section.shape[0], virt_count * col_count)
    folded = lax.dot_general(
        flat, kernel, (((1,), (1,)), ((), ())), preferred_element_type=jnp.float32
    )
    summed = settle(
        folded.reshape(tile_count, pair_count, local_pairs, window_count * row_count)
    )
    residual = (
        summed.reshape(tile_count, local_pairs, window_count, row_count)
        .transpose(1, 2, 0, 3)
        .reshape(local_pairs, window_count, virt_count)
    )
    occupied_sum = lookup(occupied_energy, pair_list[:, 0]) + lookup(
        occupied_energy, pair_list[:, 1]
    )
    window_energy = lookup(virtual_energy, window_offsets)
    denominator = (
        window_energy[None, :, None] + virtual_energy[None, None, :] - occupied_sum[:, None, None]
    )
    update = residual / denominator
    return (residual, update)


def solution(mesh):
    return jax.shard_map(
        local,
        mesh=mesh,
        in_specs=(
            P(("pair", "vtile"), None, None),
            P("vtile", "pair", None),
            P(("pair", "vtile"), None),
            P(),
            P(),
            P(),
        ),
        out_specs=(P(("pair", "vtile"), None, None), P(("pair", "vtile"), None, None)),
        check_vma=False,
    )
```

```python
import functools

import jax
import jax.numpy as jnp
from jax import lax
from jax.experimental import pallas as pl
from jax.experimental.pallas import tpu as pltpu
from jax.sharding import PartitionSpec as P

MESH = pl.DeviceIdType.MESH


def lookup(table, indices):
    positions = jnp.arange(table.shape[0], dtype=jnp.int32)
    return jnp.sum(jnp.where(positions[None, :] == indices[:, None], table[None, :], 0.0), axis=1)


def spread_kernel(
    pair_count, tile_count, sub,
    rows_ref, amp_ref, full_ref, mine_ref,
    core_buf, own_buf, up_buf, down_buf, up_out, down_out,
    core_sems, up_sems, down_sems, peer_sems, fwd_sems, amp_sems, local_sem,
):
    p = lax.axis_index("pair")
    t = lax.axis_index("vtile")
    core = lax.rem(t, 2)
    stage = t // 2
    stages = tile_count // 2
    window, cols, aux = rows_ref.shape
    half = aux // 2
    mate = (p, stage * 2 + (1 - core))
    above = (p, t + 2)
    below = (p, t - 2)
    peers = [(lax.rem(p + j, pair_count), t) for j in range(1, pair_count)]
    sources = [lax.rem(p + pair_count - j, pair_count) for j in range(1, pair_count)]

    barrier = pltpu.get_barrier_semaphore()
    around = [(p, lax.rem(t + 2, tile_count)), (p, lax.rem(t + tile_count - 2, tile_count))]
    for device in [mate] + peers + around:
        pl.semaphore_signal(barrier, inc=1, device_id=device, device_id_type=MESH)
    pl.semaphore_wait(barrier, pair_count + 2)

    mine_lanes = pl.ds(pl.multiple_of(core * half, half), half)
    mate_lanes = pl.ds(pl.multiple_of((1 - core) * half, half), half)
    chunks = [(k, pl.ds(s * sub, sub)) for k in range(window) for s in range(cols // sub)]
    count = len(chunks)

    def remote(src, dst, sems, index, device):
        return pltpu.make_async_remote_copy(
            src_ref=src, dst_ref=dst, send_sem=sems.at[(0,) + index], recv_sem=sems.at[(1,) + index],
            device_id=device, device_id_type=MESH,
        )

    def core_copy(h):
        k, rows = chunks[h]
        return remote(rows_ref.at[k, rows, mate_lanes], core_buf.at[k, rows], core_sems, (h,), mate)

    def up_copy(h):
        k, rows = chunks[h]
        return remote(up_out.at[k, rows], up_buf.at[k, rows], up_sems, (h,), above)

    def down_copy(h):
        k, rows = chunks[h]
        return remote(down_out.at[k, rows], down_buf.at[k, rows], down_sems, (h,), below)

    def peer_copy(h, j):
        k, rows = chunks[h]
        place = full_ref.at[k, p, rows, mine_lanes]
        return remote(place, place, peer_sems, (j, h), peers[j])

    def fwd_copy(h, j):
        k, rows = chunks[h]
        source = p if j == pair_count - 1 else sources[j]
        place = full_ref.at[k, source, rows, mine_lanes]
        return remote(place, place, fwd_sems, (j, h), mate)

    def amp_copy(j):
        return remote(amp_ref.at[peers[j][0]], mine_ref.at[p], amp_sems, (j,), peers[j])

    for h in range(count):
        core_copy(h).start()
    for j in range(pair_count - 1):
        amp_copy(j).start()
    keep = pltpu.make_async_copy(amp_ref.at[p], mine_ref.at[p], local_sem)
    keep.start()

    def combine(h):
        k, rows = chunks[h]
        core_copy(h).wait_recv()
        own_buf[k, rows, :] = rows_ref[k, rows, mine_lanes] + core_buf[k, rows, :]

        @pl.when(stage == 0)
        def _():
            up_out[k, rows, :] = own_buf[k, rows, :]
            up_copy(h).start()

        @pl.when(stage == stages - 1)
        def _():
            down_out[k, rows, :] = own_buf[k, rows, :]
            down_copy(h).start()

    def go_up(h):
        k, rows = chunks[h]

        @pl.when(stage > 0)
        def _():
            up_copy(h).wait_recv()

            @pl.when(stage < stages - 1)
            def _():
                up_out[k, rows, :] = own_buf[k, rows, :] + up_buf[k, rows, :]
                up_copy(h).start()

    def go_down(h):
        k, rows = chunks[h]

        @pl.when(stage < stages - 1)
        def _():
            down_copy(h).wait_recv()

            @pl.when(stage > 0)
            def _():
                down_out[k, rows, :] = own_buf[k, rows, :] + down_buf[k, rows, :]
                down_copy(h).start()

    def finish(h):
        k, rows = chunks[h]

        @pl.when(stage == 0)
        def _():
            full_ref[k, p, rows, mine_lanes] = own_buf[k, rows, :] + down_buf[k, rows, :]

        @pl.when(stage == stages - 1)
        def _():
            full_ref[k, p, rows, mine_lanes] = own_buf[k, rows, :] + up_buf[k, rows, :]

        @pl.when(jnp.logical_and(stage > 0, stage < stages - 1))
        def _():
            full_ref[k, p, rows, mine_lanes] = (
                own_buf[k, rows, :] + up_buf[k, rows, :] + down_buf[k, rows, :]
            )

        for j in range(pair_count - 1):
            peer_copy(h, j).start()
        fwd_copy(h, pair_count - 1).start()

    def forward(h):
        for j in range(pair_count - 1):
            peer_copy(h, j).wait_recv()
            fwd_copy(h, j).start()

    lower = stage < stages // 2
    ahead, lag = 2, 3

    def early(h):
        @pl.when(lower)
        def _():
            go_up(h)

        @pl.when(jnp.logical_not(lower))
        def _():
            go_down(h)

    def late(h):
        @pl.when(lower)
        def _():
            go_down(h)

        @pl.when(jnp.logical_not(lower))
        def _():
            go_up(h)

    for h in range(count):
        combine(h)
    for step in range(-ahead, count + lag):
        if 0 <= step + ahead < count:
            early(step + ahead)
        if 0 <= step < count:
            late(step)
            finish(step)
        if step >= lag:
            forward(step - lag)
    for h in range(count):
        core_copy(h).wait_send()

        @pl.when(stage < stages - 1)
        def _():
            up_copy(h).wait_send()

        @pl.when(stage > 0)
        def _():
            down_copy(h).wait_send()

        for j in range(pair_count - 1):
            peer_copy(h, j).wait_send()
        for j in range(pair_count):
            fwd_copy(h, j).wait()
    for j in range(pair_count - 1):
        amp_copy(j).wait()
    keep.wait()


def spread(picked, amp, pair_count, tile_count):
    window, cols, aux = picked.shape
    half = aux // 2
    sub = max(16, cols // 4)
    count = window * cols // sub
    block = pltpu.VMEM((window, cols, half), picked.dtype)
    dma = pltpu.SemaphoreType.DMA
    vmem = pl.BlockSpec(memory_space=pltpu.VMEM)
    return pl.pallas_call(
        functools.partial(spread_kernel, pair_count, tile_count, sub),
        out_shape=(
            jax.ShapeDtypeStruct((window, pair_count, cols, aux), picked.dtype),
            jax.ShapeDtypeStruct(amp.shape, amp.dtype),
        ),
        in_specs=[vmem, vmem],
        out_specs=(vmem, vmem),
        scratch_shapes=[block] * 6
        + [
            dma((2, count)), dma((2, count)), dma((2, count)),
            dma((2, pair_count - 1, count)), dma((2, pair_count, count)),
            dma((2, pair_count - 1)), dma,
        ],
        compiler_params=pltpu.CompilerParams(
            collective_id=0, has_side_effects=True, vmem_limit_bytes=32 * 1024 * 1024
        ),
    )(picked, amp)


def fold_kernel(amp_ref, int_ref, out_ref, amp_wide, int_wide):
    @pl.when(pl.program_id(0) == 0)
    def _():
        out_ref[...] = jnp.zeros_like(out_ref)

    amp_wide[...] = amp_ref[...].astype(jnp.float32)
    int_wide[...] = int_ref[...].astype(jnp.float32)
    total = out_ref[...]
    for c in range(0, amp_ref.shape[1], 2):
        left = jnp.concatenate([amp_wide[:, c, :], amp_wide[:, c + 1, :]], axis=1)
        right = jnp.concatenate([int_wide[:, c, :], int_wide[:, c + 1, :]], axis=1)
        total += lax.dot_general(
            left.astype(jnp.bfloat16),
            right.astype(jnp.bfloat16),
            (((1,), (1,)), ((), ())),
            preferred_element_type=jnp.float32,
        )
    out_ref[...] = total


def fold(section, integrals):
    pairs, virt, cols = section.shape
    slots = integrals.shape[0]
    block = 32
    return pl.pallas_call(
        fold_kernel,
        grid=(virt // block,),
        out_shape=jax.ShapeDtypeStruct((pairs, slots), jnp.float32),
        in_specs=[
            pl.BlockSpec((pairs, block, cols), lambda i: (0, i, 0)),
            pl.BlockSpec((slots, block, cols), lambda i: (0, i, 0)),
        ],
        out_specs=pl.BlockSpec((pairs, slots), lambda i: (0, 0)),
        scratch_shapes=[
            pltpu.VMEM((pairs, block, cols), jnp.float32),
            pltpu.VMEM((slots, block, cols), jnp.float32),
        ],
        compiler_params=pltpu.CompilerParams(vmem_limit_bytes=56 * 1024 * 1024),
        cost_estimate=pl.CostEstimate(
            flops=2 * pairs * slots * virt * cols,
            bytes_accessed=2 * virt * cols * (pairs + slots),
            transcendentals=0,
        ),
    )(section, integrals)


def settle_kernel(pair_count, tile_count, part_ref, sum_ref, inbox, sems, local_sem):
    p = lax.axis_index("pair")
    t = lax.axis_index("vtile")
    total = pair_count * tile_count
    me = p * tile_count + t
    barrier = pltpu.get_barrier_semaphore()

    def place(offset):
        other = lax.rem(me + offset, total)
        return other // tile_count, lax.rem(other, tile_count)

    for offset in range(1, total):
        pl.semaphore_signal(barrier, inc=1, device_id=place(offset), device_id_type=MESH)
    pl.semaphore_wait(barrier, total - 1)

    def copy(offset):
        there = place(offset)
        return pltpu.make_async_remote_copy(
            src_ref=part_ref.at[there[1], there[0]], dst_ref=inbox.at[p, t],
            send_sem=sems.at[0, offset], recv_sem=sems.at[1, offset],
            device_id=there, device_id_type=MESH,
        )

    for offset in range(1, total):
        copy(offset).start()
    keep = pltpu.make_async_copy(part_ref.at[t, p], inbox.at[p, t], local_sem)
    keep.start()
    keep.wait()
    for offset in range(1, total):
        copy(offset).wait()
    added = inbox[0]
    for source in range(1, pair_count):
        added = added + inbox[source]
    sum_ref[...] = added


def settle(part):
    tile_count, pair_count, local_pairs, width = part.shape
    total = tile_count * pair_count
    vmem = pl.BlockSpec(memory_space=pltpu.VMEM)
    return pl.pallas_call(
        functools.partial(settle_kernel, pair_count, tile_count),
        out_shape=jax.ShapeDtypeStruct((tile_count, local_pairs, width), part.dtype),
        in_specs=[vmem],
        out_specs=vmem,
        scratch_shapes=[
            pltpu.VMEM((pair_count, tile_count, local_pairs, width), part.dtype),
            pltpu.SemaphoreType.DMA((2, total)),
            pltpu.SemaphoreType.DMA,
        ],
        compiler_params=pltpu.CompilerParams(collective_id=1, has_side_effects=True),
    )(part)


def local(amplitudes, factors, pair_list, window_offsets, occupied_energy, virtual_energy):
    pair_count = lax.axis_size("pair")
    tile_count = lax.axis_size("vtile")
    row_count, col_count, aux_count = factors.shape
    window_count = window_offsets.shape[0]
    local_pairs, virt_count = (amplitudes.shape[0], amplitudes.shape[1])
    local_rows = window_offsets % row_count
    owned = (window_offsets // row_count) == lax.axis_index("vtile")
    picked = jnp.stack(
        [
            lax.dynamic_index_in_dim(factors, local_rows[slot_index], 0, keepdims=False)
            for slot_index in range(window_count)
        ]
    )
    picked = jnp.where(owned[:, None, None], picked, jnp.zeros_like(picked))
    amp = amplitudes.reshape(local_pairs, virt_count, pair_count, col_count).transpose(2, 0, 1, 3)
    arows, mine = spread(picked, amp, pair_count, tile_count)
    arows = arows.reshape(window_count, virt_count, aux_count)
    mine = mine.reshape(pair_count * local_pairs, virt_count, col_count)
    section = lax.all_gather(mine, "vtile", axis=0, tiled=True)
    integrals = jnp.einsum(
        "acq,bdq->abcd", arows, factors, preferred_element_type=jnp.float32
    ).astype(jnp.bfloat16)
    folded = fold(
        section, integrals.reshape(window_count * row_count, virt_count, col_count)
    )
    summed = settle(
        folded.reshape(tile_count, pair_count, local_pairs, window_count * row_count)
    )
    residual = (
        summed.reshape(tile_count, local_pairs, window_count, row_count)
        .transpose(1, 2, 0, 3)
        .reshape(local_pairs, window_count, virt_count)
    )
    occupied_sum = lookup(occupied_energy, pair_list[:, 0]) + lookup(
        occupied_energy, pair_list[:, 1]
    )
    window_energy = lookup(virtual_energy, window_offsets)
    denominator = (
        window_energy[None, :, None] + virtual_energy[None, None, :] - occupied_sum[:, None, None]
    )
    update = residual / denominator
    return (residual, update)


def solution(mesh):
    return jax.shard_map(
        local,
        mesh=mesh,
        in_specs=(
            P(("pair", "vtile"), None, None),
            P("vtile", "pair", None),
            P(("pair", "vtile"), None),
            P(),
            P(),
            P(),
        ),
        out_specs=(P(("pair", "vtile"), None, None), P(("pair", "vtile"), None, None)),
        check_vma=False,
    )
```

```python
import functools

import jax
import jax.numpy as jnp
from jax import lax
from jax.experimental import pallas as pl
from jax.experimental.pallas import tpu as pltpu
from jax.sharding import PartitionSpec as P

MESH = pl.DeviceIdType.MESH


def lookup(table, indices):
    positions = jnp.arange(table.shape[0], dtype=jnp.int32)
    return jnp.sum(jnp.where(positions[None, :] == indices[:, None], table[None, :], 0.0), axis=1)


def spread_kernel(
    pair_count, tile_count, sub,
    rows_ref, amp_ref, full_ref, mine_ref,
    core_buf, own_buf, up_buf, down_buf, up_out, down_out,
    core_sems, up_sems, down_sems, peer_sems, fwd_sems, amp_sems, local_sem,
):
    p = lax.axis_index("pair")
    t = lax.axis_index("vtile")
    core = lax.rem(t, 2)
    stage = t // 2
    stages = tile_count // 2
    window, cols, aux = rows_ref.shape
    half = aux // 2
    mate = (p, stage * 2 + (1 - core))
    above = (p, t + 2)
    below = (p, t - 2)
    relayed = pair_count == 4
    if relayed:
        across = p + 1 - 2 * lax.rem(p, 2)
        along = lax.rem(p + 2, 4)
        sources = [across, along, lax.rem(across + 2, 4)]
        peers = [(source, t) for source in sources]
    else:
        peers = [(lax.rem(p + j, pair_count), t) for j in range(1, pair_count)]
        sources = [lax.rem(p + pair_count - j, pair_count) for j in range(1, pair_count)]
    near = 2 if relayed else pair_count - 1

    barrier = pltpu.get_barrier_semaphore()
    around = [(p, lax.rem(t + 2, tile_count)), (p, lax.rem(t + tile_count - 2, tile_count))]
    for device in [mate] + peers + around:
        pl.semaphore_signal(barrier, inc=1, device_id=device, device_id_type=MESH)
    pl.semaphore_wait(barrier, pair_count + 2)

    mine_lanes = pl.ds(pl.multiple_of(core * half, half), half)
    mate_lanes = pl.ds(pl.multiple_of((1 - core) * half, half), half)
    chunks = [(k, pl.ds(s * sub, sub)) for k in range(window) for s in range(cols // sub)]
    count = len(chunks)

    def remote(src, dst, sems, index, device):
        return pltpu.make_async_remote_copy(
            src_ref=src, dst_ref=dst, send_sem=sems.at[(0,) + index], recv_sem=sems.at[(1,) + index],
            device_id=device, device_id_type=MESH,
        )

    def core_copy(h):
        k, rows = chunks[h]
        return remote(rows_ref.at[k, rows, mate_lanes], core_buf.at[k, rows], core_sems, (h,), mate)

    def up_copy(h):
        k, rows = chunks[h]
        return remote(up_out.at[k, rows], up_buf.at[k, rows], up_sems, (h,), above)

    def down_copy(h):
        k, rows = chunks[h]
        return remote(down_out.at[k, rows], down_buf.at[k, rows], down_sems, (h,), below)

    def peer_copy(h, j):
        k, rows = chunks[h]
        if j >= near:
            place = full_ref.at[k, sources[h % 2], rows, mine_lanes]
            return remote(place, place, peer_sems, (j, h), peers[1 - h % 2])
        place = full_ref.at[k, p, rows, mine_lanes]
        return remote(place, place, peer_sems, (j, h), peers[j])

    def fwd_copy(h, j):
        k, rows = chunks[h]
        source = p if j == pair_count - 1 else sources[j]
        place = full_ref.at[k, source, rows, mine_lanes]
        return remote(place, place, fwd_sems, (j, h), mate)

    def amp_copy(j):
        return remote(amp_ref.at[peers[j][0]], mine_ref.at[p], amp_sems, (j,), peers[j])

    for h in range(count):
        core_copy(h).start()
    for j in range(pair_count - 1):
        amp_copy(j).start()
    keep = pltpu.make_async_copy(amp_ref.at[p], mine_ref.at[p], local_sem)
    keep.start()

    def combine(h):
        k, rows = chunks[h]
        core_copy(h).wait_recv()
        own_buf[k, rows, :] = rows_ref[k, rows, mine_lanes] + core_buf[k, rows, :]

        @pl.when(stage == 0)
        def _():
            up_out[k, rows, :] = own_buf[k, rows, :]
            up_copy(h).start()

        @pl.when(stage == stages - 1)
        def _():
            down_out[k, rows, :] = own_buf[k, rows, :]
            down_copy(h).start()

    def go_up(h):
        k, rows = chunks[h]

        @pl.when(stage > 0)
        def _():
            up_copy(h).wait_recv()

            @pl.when(stage < stages - 1)
            def _():
                up_out[k, rows, :] = own_buf[k, rows, :] + up_buf[k, rows, :]
                up_copy(h).start()

    def go_down(h):
        k, rows = chunks[h]

        @pl.when(stage < stages - 1)
        def _():
            down_copy(h).wait_recv()

            @pl.when(stage > 0)
            def _():
                down_out[k, rows, :] = own_buf[k, rows, :] + down_buf[k, rows, :]
                down_copy(h).start()

    def finish(h):
        k, rows = chunks[h]

        @pl.when(stage == 0)
        def _():
            full_ref[k, p, rows, mine_lanes] = own_buf[k, rows, :] + down_buf[k, rows, :]

        @pl.when(stage == stages - 1)
        def _():
            full_ref[k, p, rows, mine_lanes] = own_buf[k, rows, :] + up_buf[k, rows, :]

        @pl.when(jnp.logical_and(stage > 0, stage < stages - 1))
        def _():
            full_ref[k, p, rows, mine_lanes] = (
                own_buf[k, rows, :] + up_buf[k, rows, :] + down_buf[k, rows, :]
            )

        for j in range(near):
            peer_copy(h, j).start()
        fwd_copy(h, pair_count - 1).start()

    def forward(h):
        for j in range(near):
            peer_copy(h, j).wait_recv()
            fwd_copy(h, j).start()
            if relayed and j == h % 2:
                peer_copy(h, near).start()

    def forward_far(h):
        for j in range(near, pair_count - 1):
            peer_copy(h, j).wait_recv()
            fwd_copy(h, j).start()

    lower = stage < stages // 2
    ahead, lag = 2, 3

    def early(h):
        @pl.when(lower)
        def _():
            go_up(h)

        @pl.when(jnp.logical_not(lower))
        def _():
            go_down(h)

    def late(h):
        @pl.when(lower)
        def _():
            go_down(h)

        @pl.when(jnp.logical_not(lower))
        def _():
            go_up(h)

    for h in range(count):
        combine(h)
    for step in range(-ahead, count + 2 * lag):
        if 0 <= step + ahead < count:
            early(step + ahead)
        if 0 <= step < count:
            late(step)
            finish(step)
        if 0 <= step - lag < count:
            forward(step - lag)
        if 0 <= step - 2 * lag < count:
            forward_far(step - 2 * lag)
    for h in range(count):
        core_copy(h).wait_send()

        @pl.when(stage < stages - 1)
        def _():
            up_copy(h).wait_send()

        @pl.when(stage > 0)
        def _():
            down_copy(h).wait_send()

        for j in range(pair_count - 1):
            peer_copy(h, j).wait_send()
        for j in range(pair_count):
            fwd_copy(h, j).wait()
    for j in range(pair_count - 1):
        amp_copy(j).wait()
    keep.wait()


def spread(picked, amp, pair_count, tile_count):
    window, cols, aux = picked.shape
    half = aux // 2
    sub = max(16, cols // 4)
    count = window * cols // sub
    block = pltpu.VMEM((window, cols, half), picked.dtype)
    dma = pltpu.SemaphoreType.DMA
    vmem = pl.BlockSpec(memory_space=pltpu.VMEM)
    return pl.pallas_call(
        functools.partial(spread_kernel, pair_count, tile_count, sub),
        out_shape=(
            jax.ShapeDtypeStruct((window, pair_count, cols, aux), picked.dtype),
            jax.ShapeDtypeStruct(amp.shape, amp.dtype),
        ),
        in_specs=[vmem, vmem],
        out_specs=(vmem, vmem),
        scratch_shapes=[block] * 6
        + [
            dma((2, count)), dma((2, count)), dma((2, count)),
            dma((2, pair_count - 1, count)), dma((2, pair_count, count)),
            dma((2, pair_count - 1)), dma,
        ],
        compiler_params=pltpu.CompilerParams(
            collective_id=0, has_side_effects=True, vmem_limit_bytes=32 * 1024 * 1024
        ),
    )(picked, amp)


def fold_kernel(amp_ref, int_ref, out_ref):
    @pl.when(pl.program_id(0) == 0)
    def _():
        out_ref[...] = jnp.zeros_like(out_ref)

    pairs, block, cols = amp_ref.shape
    total = out_ref[...]
    for c in range(0, block, 16):
        left = amp_ref[:, c : c + 16, :].reshape(pairs, 16 * cols)
        right = int_ref[:, c : c + 16, :].reshape(int_ref.shape[0], 16 * cols)
        total += lax.dot_general(
            left, right, (((1,), (1,)), ((), ())), preferred_element_type=jnp.float32
        )
    out_ref[...] = total


def fold(section, integrals):
    pairs, virt, cols = section.shape
    slots = integrals.shape[0]
    block = 64
    return pl.pallas_call(
        fold_kernel,
        grid=(virt // block,),
        out_shape=jax.ShapeDtypeStruct((pairs, slots), jnp.float32),
        in_specs=[
            pl.BlockSpec((pairs, block, cols), lambda i: (0, i, 0)),
            pl.BlockSpec((slots, block, cols), lambda i: (0, i, 0)),
        ],
        out_specs=pl.BlockSpec((pairs, slots), lambda i: (0, 0)),
        compiler_params=pltpu.CompilerParams(vmem_limit_bytes=56 * 1024 * 1024),
        cost_estimate=pl.CostEstimate(
            flops=2 * pairs * slots * virt * cols,
            bytes_accessed=2 * virt * cols * (pairs + slots),
            transcendentals=0,
        ),
    )(section, integrals)


def settle_kernel(pair_count, tile_count, part_ref, sum_ref, inbox, sems, local_sem):
    p = lax.axis_index("pair")
    t = lax.axis_index("vtile")
    total = pair_count * tile_count
    me = p * tile_count + t
    barrier = pltpu.get_barrier_semaphore()

    def place(offset):
        other = lax.rem(me + offset, total)
        return other // tile_count, lax.rem(other, tile_count)

    for offset in range(1, total):
        pl.semaphore_signal(barrier, inc=1, device_id=place(offset), device_id_type=MESH)
    pl.semaphore_wait(barrier, total - 1)

    def copy(offset):
        there = place(offset)
        return pltpu.make_async_remote_copy(
            src_ref=part_ref.at[there[1], there[0]], dst_ref=inbox.at[p, t],
            send_sem=sems.at[0, offset], recv_sem=sems.at[1, offset],
            device_id=there, device_id_type=MESH,
        )

    for offset in range(1, total):
        copy(offset).start()
    keep = pltpu.make_async_copy(part_ref.at[t, p], inbox.at[p, t], local_sem)
    keep.start()
    keep.wait()
    for offset in range(1, total):
        copy(offset).wait()
    added = inbox[0]
    for source in range(1, pair_count):
        added = added + inbox[source]
    sum_ref[...] = added


def settle(part):
    tile_count, pair_count, local_pairs, width = part.shape
    total = tile_count * pair_count
    vmem = pl.BlockSpec(memory_space=pltpu.VMEM)
    return pl.pallas_call(
        functools.partial(settle_kernel, pair_count, tile_count),
        out_shape=jax.ShapeDtypeStruct((tile_count, local_pairs, width), part.dtype),
        in_specs=[vmem],
        out_specs=vmem,
        scratch_shapes=[
            pltpu.VMEM((pair_count, tile_count, local_pairs, width), part.dtype),
            pltpu.SemaphoreType.DMA((2, total)),
            pltpu.SemaphoreType.DMA,
        ],
        compiler_params=pltpu.CompilerParams(collective_id=1, has_side_effects=True),
    )(part)


def local(amplitudes, factors, pair_list, window_offsets, occupied_energy, virtual_energy):
    pair_count = lax.axis_size("pair")
    tile_count = lax.axis_size("vtile")
    row_count, col_count, aux_count = factors.shape
    window_count = window_offsets.shape[0]
    local_pairs, virt_count = (amplitudes.shape[0], amplitudes.shape[1])
    local_rows = window_offsets % row_count
    owned = (window_offsets // row_count) == lax.axis_index("vtile")
    picked = jnp.stack(
        [
            lax.dynamic_index_in_dim(factors, local_rows[slot_index], 0, keepdims=False)
            for slot_index in range(window_count)
        ]
    )
    picked = jnp.where(owned[:, None, None], picked, jnp.zeros_like(picked))
    amp = amplitudes.reshape(local_pairs, virt_count, pair_count, col_count).transpose(2, 0, 1, 3)
    arows, mine = spread(picked, amp, pair_count, tile_count)
    arows = arows.reshape(window_count, virt_count, aux_count)
    mine = mine.reshape(pair_count * local_pairs, virt_count, col_count)
    section = lax.all_gather(mine, "vtile", axis=0, tiled=True)
    integrals = jnp.einsum(
        "acq,bdq->abcd", arows, factors, preferred_element_type=jnp.float32
    ).astype(jnp.bfloat16)
    folded = fold(
        section, integrals.reshape(window_count * row_count, virt_count, col_count)
    )
    summed = settle(
        folded.reshape(tile_count, pair_count, local_pairs, window_count * row_count)
    )
    residual = (
        summed.reshape(tile_count, local_pairs, window_count, row_count)
        .transpose(1, 2, 0, 3)
        .reshape(local_pairs, window_count, virt_count)
    )
    occupied_sum = lookup(occupied_energy, pair_list[:, 0]) + lookup(
        occupied_energy, pair_list[:, 1]
    )
    window_energy = lookup(virtual_energy, window_offsets)
    denominator = (
        window_energy[None, :, None] + virtual_energy[None, None, :] - occupied_sum[:, None, None]
    )
    update = residual / denominator
    return (residual, update)


def solution(mesh):
    return jax.shard_map(
        local,
        mesh=mesh,
        in_specs=(
            P(("pair", "vtile"), None, None),
            P("vtile", "pair", None),
            P(("pair", "vtile"), None),
            P(),
            P(),
            P(),
        ),
        out_specs=(P(("pair", "vtile"), None, None), P(("pair", "vtile"), None, None)),
        check_vma=False,
    )
```
